32 devices in a mesh: rep: 2 (over core), grp: 16 (over z, y, x).
Axes of the slice: x: 2, y: 2, z: 4, core: 2. Of those that a mesh axis runs over, the one named last changes fastest.
Arguments:
- tokens: bfloat16 [4096, 2048], P(('rep', 'grp')), may hold values from -6 to 6
- cotangent: bfloat16 [4096, 2048], P(('rep', 'grp')), may hold values from -6 to 6
- lengths: int32 [32, 4], replicated, may hold values from 1 to 80, 128 in all within a row
- dealing: int32 [32], replicated, may hold values from 0 to 31, each once
- routes: int32 [4096, 8], P(('rep', 'grp')), may hold values from 0 to 15, all different within a row; in each aligned block of 128 rows (0 to 127, 128 to 255, ...) at most 96 rows name the same one
- gate_weights: float32 [4096, 8], P(('rep', 'grp')), may hold values from 0.05 to 0.25
- pair_order: int32 [4096, 8], P(('rep', 'grp')), may hold values from 0 to 1023, as said below
- qkv_weight: bfloat16 [2048, 5120], P('grp'), may hold values from -0.125 to 0.125
- out_weight: bfloat16 [4096, 2048], P('grp'), may hold values from -0.25 to 0.25
- input_gain: bfloat16 [2048], P('grp'), may hold values from 0.5 to 1.5
- query_gain: bfloat16 [128], P('grp'), may hold values from 0.5 to 1.5
- key_gain: bfloat16 [128], P('grp'), may hold values from 0.5 to 1.5
- post_gain: bfloat16 [2048], P('grp'), may hold values from 0.5 to 1.5
- gate_weight: bfloat16 [16, 2048, 768], P('grp'), may hold values from -0.125 to 0.125
- up_weight: bfloat16 [16, 2048, 768], P('grp'), may hold values from -0.125 to 0.125
- down_weight: bfloat16 [16, 768, 2048], P('grp'), may hold values from -0.4375 to 0.4375
Outputs:
- output: bfloat16 [4096, 2048], P(('rep', 'grp'))
- input_grad: float32 [4096, 2048], P(('rep', 'grp'))
- qkv_grad: float32 [2048, 5120], P('grp')
- out_grad: float32 [4096, 2048], P('grp')
- input_gain_grad: float32 [2048], P('grp')
- query_gain_grad: float32 [128], P('grp')
- key_gain_grad: float32 [128], P('grp')
- post_gain_grad: float32 [2048], P('grp')
- gate_grad: float32 [16, 2048, 768], P('grp')
- up_grad: float32 [16, 2048, 768], P('grp')
- down_grad: float32 [16, 768, 2048], P('grp')
The draws below stay inside these ranges and needn't reach their ends.
Inputs may be any that keep to these rules, and one draw needn't show every extreme that they name: In the rows of one device, no expert is named by more than 96 routes, and a token names an expert at most once. `pair_order`: within the rows of each device, the 1024 entries are each number once. `lengths`: each row sums to 128. `dealing`: each pack once.
All inputs are finite; a program needn't handle non-finite values.
Results may differ from the reference program's by a relative error of at most 0.019.
Values may be sent and summed in bfloat16 or wider, within the bound.
No kernel may reach another device: no remote copies, remote signals or barrier semaphores. Data moves between devices by JAX's collectives and lax.ppermute only.
A program may use at most 256 MiB of HBM per device.

```python
import math
import jax
import jax.numpy as jnp
import numpy as np
from jax import lax

D = 2048
HEADS = 32
KV_HEADS = 4
HEAD_DIM = 128
FF = 768
TOP = 8
TOK_DEV = 128
SEQ_PACK = 4
EXPERTS = 16
TOKENS = 4096
PACKS = 32
SEND_MOST = 96
CAPACITY = 1280
LEN_MAX = 80
N_REP = 2
N_GRP = 16


def draw_pair_order(key, part):
    blocks = TOKENS // TOK_DEV
    subkeys = jax.random.split(key, blocks)
    ranked = jax.vmap(lambda single: jax.random.permutation(single, TOK_DEV * TOP))(subkeys)
    return ranked.reshape(TOKENS, TOP).astype(jnp.int32)


def levels(stream_key, shape, shards, smallest, high):
    def one(dim, shards_of):
        heights = jax.random.uniform(jax.random.fold_in(jax.random.fold_in(stream_key, 6), dim), (shards_of,), jnp.float32, smallest / len(shards), high / len(shards))
        return jnp.repeat(jnp.exp(heights), shape[dim] // shards_of).reshape((-1,) + (1,) * (len(shape) - dim - 1))

    level = one(*shards[0])
    for cut in shards[1:]:
        level = level * one(*cut)
    return level


def length_profile(number_of, total, reach, slope):
    loads = [(1 << 20) // math.isqrt(standing ** slope) + 1 for standing in range(2, number_of + 1)]
    rest, holding = total - reach - (number_of - 1), [1] * (number_of - 1)
    while rest > 0:
        free = [i for i in range(number_of - 1) if holding[i] < reach]
        mass, left = sum([loads[i] for i in free]), rest
        for i in free:
            more = min(reach - holding[i], max(1, left * loads[i] // mass), rest)
            holding[i] = holding[i] + more
            rest = rest - more
    return np.array([reach] + holding)


def uneven(key, count, total, bound, skew):
    if count == 2:
        one = jax.random.randint(key, (), max(1, total - bound), min(bound, total - 1) + 1)
        return jnp.stack([one, total - one])
    sizes = jnp.asarray(length_profile(count, total, bound, skew), jnp.int32)
    couples = (count - 1) // 2
    giver, sink = sizes[1:1 + 2 * couples:2], sizes[2:2 + 2 * couples:2]
    margin = jnp.minimum(giver - 1, bound - sink)
    shifted = jax.random.randint(jax.random.fold_in(key, 1), (couples,), 0, 1 << 20) % (margin + 1)
    sizes = sizes.at[1:1 + 2 * couples:2].set(giver - shifted).at[2:2 + 2 * couples:2].set(sink + shifted)
    return sizes[jax.random.permutation(jax.random.fold_in(key, 2), count)]


def shared_out(own_key, own, number, rows, count, top, most, skew):
    order = jax.random.permutation(own_key, count)
    heavy_load, usual = load_shares(count, rows * top, most, skew, True), load_shares(count, rows * top, most, skew, False)
    places = jnp.arange(count)

    def named(sizes, turn):
        used = int((sizes > 0).sum())
        fixed = max(1, used // 4)
        moved = fixed + (places - fixed + turn * (used - fixed)) % max(1, count - fixed)
        return jnp.zeros((count,), jnp.int32).at[order[jnp.where(places < fixed, places, moved)]].set(jnp.asarray(sizes, jnp.int32))

    sizes = jnp.where(number % 4 == 0, named(heavy_load, number // 4), named(usual, number - number // 4 - 1))
    mixed = jax.random.permutation(jax.random.fold_in(own, 3), count)
    source_of, taker = mixed[0:count // 2 * 2:2], mixed[1:count // 2 * 2:2]
    room = jnp.minimum(sizes[source_of] - 1, most - sizes[taker]) // 2
    room = jnp.where((source_of == order[0]) | (taker == order[0]) | (sizes[taker] == 0), 0, jnp.maximum(room, 0))
    moved = jax.random.randint(jax.random.fold_in(own, 4), (count // 2,), 0, 1 << 20) % (room + 1)
    sizes = sizes.at[source_of].add(-moved).at[taker].add(moved)
    items = jnp.searchsorted(jnp.cumsum(sizes), jnp.arange(rows * top), side="right").astype(jnp.int32)
    listing = items.reshape(top, rows).T
    listing = listing[jax.random.permutation(jax.random.fold_in(own, 1), rows)]
    turn = jax.random.randint(jax.random.fold_in(own, 2), (rows, 1), 0, top)
    return jnp.take_along_axis(listing, (jnp.arange(top)[None, :] + turn) % top, axis=1)


def load_shares(amount, total, most, skew, full):
    weights = [(1 << 20) // math.isqrt(grade ** skew) + 1 for grade in range(1, amount + 1)]
    largest = most if full else min(most, max(-(-total // amount), total * weights[0] // sum(weights)))
    least = 1 if total - largest >= amount - 1 else 0
    holding, spare = [largest] + [least] * (amount - 1), total - largest - least * (amount - 1)
    while spare > 0:
        candidates = [i for i in range(1, amount) if holding[i] < largest] or [i for i in range(1, amount) if holding[i] < most]
        mass, remaining = sum([weights[i] for i in candidates]), spare
        for i in candidates:
            extra = min(most - holding[i], max(1, remaining * weights[i] // mass), spare)
            holding[i] = holding[i] + extra
            spare = spare - extra
    return np.array(holding)


def normal_values(stream_key, extent, width, most, pieces=(), kind=jnp.bfloat16):
    array = width * jax.random.normal(stream_key, extent, jnp.float32)
    if pieces:
        array = array * levels(stream_key, extent, pieces, -0.22, 0.18)
    return jnp.clip(array, -most, most).astype(kind)


def setup_inputs(seed: int = 0) -> dict:
    key_list = jax.random.split(jax.random.key(seed), 17)
    tokens = normal_values(key_list[0], (TOKENS, D), 1.0, 6.0, ((0, 32),))
    cotangent = normal_values(key_list[1], (TOKENS, D), 1.0, 6.0, ((0, 32),))
    lengths = jax.vmap(lambda own: uneven(own, SEQ_PACK, TOK_DEV, LEN_MAX, 2))(jax.random.split(key_list[2], PACKS)).reshape((PACKS, SEQ_PACK)).astype(jnp.int32)
    dealing = jax.random.permutation(key_list[3], PACKS).astype(jnp.int32)
    routes_keys = jax.random.split(jax.random.fold_in(key_list[4], 1), TOKENS // TOK_DEV)
    routes_turns = jax.random.permutation(jax.random.fold_in(key_list[4], 3), TOKENS // TOK_DEV)
    routes = jax.vmap(lambda own, number: shared_out(jax.random.fold_in(key_list[4], 2), own, number, TOK_DEV, EXPERTS, TOP, SEND_MOST, 2))(routes_keys, routes_turns).reshape((TOKENS, TOP))
    gate_weights = jnp.clip(0.05 + 0.2 * jax.random.uniform(key_list[5], (TOKENS, TOP), jnp.float32) ** levels(key_list[5], (TOKENS, TOP), ((0, 32),), -0.2, 0.2), 0.05, 0.25)
    pair_order = draw_pair_order(jax.random.fold_in(key_list[16], 71), 0)
    qkv_weight = normal_values(key_list[7], (D, (HEADS + 2 * KV_HEADS) * HEAD_DIM), D ** -0.5, 0.125, ((0, 16),))
    out_weight = normal_values(key_list[8], (HEADS * HEAD_DIM, D), (HEADS * HEAD_DIM // 8) ** -0.5, 0.25, ((0, 16),))
    input_gain = jnp.clip(1.0 + 0.1 * jax.random.normal(key_list[9], (D,), jnp.float32), 0.5, 1.5).astype(jnp.bfloat16)
    query_gain = jnp.clip(1.0 + 0.1 * jax.random.normal(key_list[10], (HEAD_DIM,), jnp.float32), 0.5, 1.5).astype(jnp.bfloat16)
    key_gain = jnp.clip(1.0 + 0.1 * jax.random.normal(key_list[11], (HEAD_DIM,), jnp.float32), 0.5, 1.5).astype(jnp.bfloat16)
    post_gain = jnp.clip(1.0 + 0.1 * jax.random.normal(key_list[12], (D,), jnp.float32), 0.5, 1.5).astype(jnp.bfloat16)
    gate_weight = normal_values(key_list[13], (EXPERTS, D, FF), D ** -0.5, 0.125, ((0, 16),))
    up_weight = normal_values(key_list[14], (EXPERTS, D, FF), D ** -0.5, 0.125, ((0, 16),))
    down_weight = normal_values(key_list[15], (EXPERTS, FF, D), (FF // 4) ** -0.5, 0.4375, ((0, 16),))
    return {"tokens": tokens, "cotangent": cotangent, "lengths": lengths, "dealing": dealing, "routes": routes, "gate_weights": gate_weights, "pair_order": pair_order, "qkv_weight": qkv_weight, "out_weight": out_weight, "input_gain": input_gain, "query_gain": query_gain, "key_gain": key_gain, "post_gain": post_gain, "gate_weight": gate_weight, "up_weight": up_weight, "down_weight": down_weight}


EPSILON = 1e-06
ROPE_BASE = 1000000.0
HIGHEST = lax.Precision.HIGHEST

@jax.custom_vjp
def low(v):
    return lax.optimization_barrier(v.astype(jnp.bfloat16)).astype(jnp.float32)

@jax.custom_vjp
def low_back(v):
    return v

def low_keep(v):
    return (low(v), None)

def low_pass(kept, grad):
    return (grad,)

def back_keep(v):
    return (v, None)

def back_low(kept, grad):
    return (low(grad),)
low.defvjp(low_keep, low_pass)
low_back.defvjp(back_keep, back_low)

def product(left, right):
    return jnp.dot(left, right, precision=HIGHEST, preferred_element_type=jnp.float32)

def rms_rows(values):
    return lax.rsqrt(lax.optimization_barrier(jnp.mean(values * values, axis=-1, keepdims=True)) + EPSILON)

def layout(length_row):
    ends = jnp.cumsum(length_row).astype(jnp.int32)
    places = jnp.arange(TOK_DEV, dtype=jnp.int32)
    segment = lax.optimization_barrier(jnp.sum((places[:, None] >= ends[None, :]).astype(jnp.int32), axis=1)).astype(jnp.int32)
    starts = (ends - length_row).astype(jnp.int32)
    position = (places - jnp.take(starts, segment)).astype(jnp.int32)
    return (segment, position)

def rope_tables(position):
    half = HEAD_DIM // 2
    freq = ROPE_BASE ** (-jnp.arange(half, dtype=jnp.float32) * 2.0 / HEAD_DIM)
    angle = position.astype(jnp.float32)[:, None] * freq[None, :]
    cosine = jnp.concatenate([jnp.cos(angle), jnp.cos(angle)], axis=1)
    sine = jnp.concatenate([jnp.sin(angle), jnp.sin(angle)], axis=1)
    return (cosine, sine)

def rotate(values, cosine, sine):
    half = values.shape[-1] // 2
    turned = jnp.concatenate([-values[..., half:], values[..., :half]], axis=-1)
    return values * cosine[:, None, :] + turned * sine[:, None, :]

def local_places(route_row, order_row):
    pairs = route_row.shape[0]
    inverse = jnp.zeros((pairs,), jnp.int32).at[order_row].set(jnp.arange(pairs, dtype=jnp.int32))
    ordered = jnp.take(route_row, inverse)
    table = (ordered[:, None] == jnp.arange(EXPERTS, dtype=jnp.int32)[None, :]).astype(jnp.int32)
    before = (jnp.cumsum(table, axis=0) - table).astype(jnp.int32)
    rank_sorted = lax.optimization_barrier(jnp.sum(before * table, axis=1)).astype(jnp.int32)
    return (jnp.take(rank_sorted, order_row), lax.optimization_barrier(jnp.sum(table, axis=0)).astype(jnp.int32))

def attend(item):
    queries, keys, values, segment = item
    count = queries.shape[0]
    grouped = queries.reshape(count, KV_HEADS, HEADS // KV_HEADS, HEAD_DIM)
    raw = jnp.einsum('ikgd,jkd->kgij', grouped, keys, precision=HIGHEST)
    scores = low_back(raw * HEAD_DIM ** (-0.5))
    places = jnp.arange(count, dtype=jnp.int32)
    allowed = (segment[:, None] == segment[None, :]) & (places[None, :] <= places[:, None])
    scores = jnp.where(allowed, scores, -1e+30)
    prob = jax.nn.softmax(scores, axis=-1)
    mixed = jnp.einsum('kgij,jkd->ikgd', low(prob), values, precision=HIGHEST)
    return mixed.reshape(count, HEADS * HEAD_DIM)

def reference(tokens, cotangent, lengths, dealing, routes, gate_weights, pair_order, qkv_weight, out_weight, input_gain, query_gain, key_gain, post_gain, gate_weight, up_weight, down_weight):
    packs = N_REP * N_GRP
    pairs = TOK_DEV * TOP
    rows_used = jnp.take(lengths, dealing, axis=0)
    segment, position = jax.vmap(layout)(rows_used)
    cosine, sine = rope_tables(position.reshape(TOKENS))
    route_rows = routes.reshape(packs, pairs)
    ranks, counts = jax.vmap(local_places)(route_rows, pair_order.reshape(packs, pairs))
    per_replica = counts.reshape(N_REP, N_GRP, EXPERTS)
    base = (jnp.cumsum(per_replica, axis=1) - per_replica).astype(jnp.int32).reshape(packs, EXPERTS)
    kept = jnp.take_along_axis(base, route_rows, axis=1) + ranks < CAPACITY
    device = jnp.arange(packs, dtype=jnp.int32)[:, None]
    slot_rows = N_GRP * SEND_MOST
    total_slots = N_REP * EXPERTS * slot_rows
    target = ((device // N_GRP * EXPERTS + route_rows) * N_GRP + device % N_GRP) * SEND_MOST + ranks
    target = jnp.where(kept, target, total_slots).astype(jnp.int32).reshape(-1)
    owner_token = (device * TOK_DEV + jnp.arange(pairs, dtype=jnp.int32)[None, :] // TOP).astype(jnp.int32).reshape(-1)
    slot_token = jnp.full((total_slots,), TOKENS, jnp.int32).at[target].set(owner_token, mode='drop').reshape(N_REP * EXPERTS, slot_rows)
    slot_weight = jnp.zeros((total_slots,), gate_weights.dtype).at[target].set(gate_weights.reshape(-1), mode='drop').reshape(N_REP * EXPERTS, slot_rows)
    slot_expert = (jnp.arange(N_REP * EXPERTS, dtype=jnp.int32) % EXPERTS).astype(jnp.int32)
    qsize = HEADS * HEAD_DIM
    ksize = KV_HEADS * HEAD_DIM

    def forward(inputs, qkv_matrix, out_matrix, in_gain, q_gain, k_gain, p_gain, gate_matrix, up_matrix, down_matrix):
        normed = low(inputs * rms_rows(inputs) * in_gain)
        projected = low_back(product(normed, qkv_matrix))
        q_raw = projected[:, :qsize].reshape(TOKENS, HEADS, HEAD_DIM)
        k_raw = projected[:, qsize:qsize + ksize].reshape(TOKENS, KV_HEADS, HEAD_DIM)
        v_raw = projected[:, qsize + ksize:].reshape(TOKENS, KV_HEADS, HEAD_DIM)
        queries = low(rotate(q_raw * rms_rows(q_raw) * q_gain, cosine, sine))
        keys = low(rotate(k_raw * rms_rows(k_raw) * k_gain, cosine, sine))
        values = low(v_raw)
        mixed = lax.map(jax.checkpoint(attend), (queries.reshape(packs, TOK_DEV, HEADS, HEAD_DIM), keys.reshape(packs, TOK_DEV, KV_HEADS, HEAD_DIM), values.reshape(packs, TOK_DEV, KV_HEADS, HEAD_DIM), segment))
        mixed = low(low_back(mixed.reshape(TOKENS, qsize)))
        resid = inputs + low_back(product(mixed, out_matrix))
        routed = low(resid * rms_rows(resid) * p_gain)
        padded = jnp.concatenate([routed, jnp.zeros((1, D), routed.dtype)], axis=0)

        def expert_block(item):
            token_ids, slot_scale, expert_id = item
            rows = low_back(jnp.take(padded, token_ids, axis=0))
            gate = low_back(product(rows, jnp.take(gate_matrix, expert_id, axis=0)))
            upper = low_back(product(rows, jnp.take(up_matrix, expert_id, axis=0)))
            hidden = low(jax.nn.silu(gate) * upper)
            result = low(low_back(product(hidden, jnp.take(down_matrix, expert_id, axis=0))))
            return result * slot_scale[:, None]
        weighted = lax.map(jax.checkpoint(expert_block), (slot_token, slot_weight, slot_expert))
        mixture = jnp.zeros((TOKENS + 1, D), routed.dtype).at[slot_token.reshape(-1)].add(weighted.reshape(-1, D))
        return resid + mixture[:TOKENS]
    result, pullback = jax.vjp(forward, tokens.astype(jnp.float32), qkv_weight.astype(jnp.float32), out_weight.astype(jnp.float32), input_gain.astype(jnp.float32), query_gain.astype(jnp.float32), key_gain.astype(jnp.float32), post_gain.astype(jnp.float32), gate_weight.astype(jnp.float32), up_weight.astype(jnp.float32), down_weight.astype(jnp.float32))
    grads = pullback(cotangent.astype(jnp.float32))
    return (result.astype(jnp.bfloat16), grads[0], grads[1], grads[2], grads[3], grads[4], grads[5], grads[6], grads[7], grads[8], grads[9])
```

```python
import jax
import jax.numpy as jnp
from jax import lax
from jax.sharding import PartitionSpec as P

D = 2048
HEADS = 32
KV_HEADS = 4
HEAD_DIM = 128
FF = 768
TOP = 8
CAPACITY = 1280
LINE = 4
EXPERT_ROWS = 1024

EPSILON = 1e-06
ROPE_BASE = 1000000.0
AXES = ("rep", "grp")
F32 = jnp.float32
BF16 = jnp.bfloat16


class Wires:
    def __init__(self):
        self.groups = lax.axis_size("grp")
        self.plane = self.groups // LINE
        self.bits = self.plane.bit_length() - 1
        self.rep = lax.axis_index("rep")
        self.group = lax.axis_index("grp")
        self.line = self.group // self.plane
        self.spot = self.group % self.plane

    def moved(self, value, pairs):
        return lax.ppermute(value, AXES, pairs)

    def pairs(self, where):
        found = []
        for r in range(2):
            for g in range(self.groups):
                to = where(r, g)
                if to is not None:
                    found.append((r * self.groups + g, to[0] * self.groups + to[1]))
        return found

    def swap(self, value, bit):
        last = self.bits - 1
        return self.moved(value, self.pairs(lambda r, g: (r, g ^ (1 << (bit if r == 0 else last - bit)))))

    def other(self, value):
        return self.moved(value, self.pairs(lambda r, g: (1 - r, g)))

    def along(self, value, step, first, final):
        def to(r, g):
            here = g // self.plane
            if first <= here <= final:
                return (r, g + step * self.plane)
            return None

        return self.moved(value, self.pairs(to))

    def line_gather(self, value):
        lower, upper = [value], [value]
        for t in range(1, LINE):
            lower.append(self.along(lower[-1], 1, t - 1, LINE - 2))
            upper.append(self.along(upper[-1], -1, 1, LINE - t))
        row = jnp.stack(lower[:0:-1] + upper, axis=0)
        return lax.dynamic_slice_in_dim(row, LINE - 1 - self.line, LINE, axis=0)

    def line_scatter(self, value):
        def piece(j):
            place = jnp.clip(self.line + j, 0, LINE - 1)
            return lax.dynamic_index_in_dim(value, place, 0, keepdims=False).astype(F32)

        total = piece(0)
        for way in (1, -1):
            carried = None
            for t in range(LINE - 1, 0, -1):
                part = piece(way * t)
                if carried is not None:
                    part = part + carried
                if way == 1:
                    first, final = (0, LINE - 1 - t)
                else:
                    first, final = (t, LINE - 1)
                carried = self.along(part.astype(BF16), way, first, final).astype(F32)
            total = total + carried
        return total

    def plane_gather(self, value):
        for bit in range(self.bits):
            value = jnp.stack([value, self.swap(value, bit)], axis=0)
        return value.reshape((self.plane,) + value.shape[self.bits :])

    def plane_scatter(self, own, other):
        for bit in reversed(range(self.bits)):
            arrived = self.swap(other.astype(BF16), bit)
            value = own.astype(F32) + arrived.astype(F32)
            half = value.shape[0] // 2
            own, other = (value[:half], value[half:])
        return value[0]

    def plane_swap(self, value):
        rest = value.shape[1:]
        value = value.reshape((2,) * self.bits + rest)
        for bit in range(self.bits):
            axis = self.bits - 1 - bit
            kept = lax.index_in_dim(value, 0, axis, keepdims=False)
            sent = lax.index_in_dim(value, 1, axis, keepdims=False)
            value = jnp.stack([kept, self.swap(sent, bit)], axis=axis)
        return value.reshape((self.plane,) + rest)

    def turned(self, number):
        back = sum(((number >> i) & 1) << (self.bits - 1 - i) for i in range(self.bits))
        return jnp.where(self.rep == 0, number, back)

    def by_relative(self, value, axis):
        return jnp.stack(
            [
                lax.dynamic_index_in_dim(value, self.spot ^ self.turned(k), axis, keepdims=False)
                for k in range(self.plane)
            ],
            axis=0,
        )

    def by_spot(self, value, axis):
        return jnp.stack(
            [
                lax.dynamic_index_in_dim(value, self.turned(self.spot ^ q), 0, keepdims=False)
                for q in range(self.plane)
            ],
            axis=axis,
        )

    def own_first(self, value, axis):
        return jnp.where(self.rep == 0, value, jnp.flip(value, axis))

    def gather(self, value):
        return self.plane_gather(self.line_gather(value))

    def gather_halves(self, value):
        value = self.line_gather(value)
        for bit in range(self.bits - 1):
            value = jnp.concatenate([value, self.swap(value, bit)], axis=0)
        value = value.reshape(-1, value.shape[-1])
        return (value, self.swap(value, self.bits - 1))

    def scatter(self, own, other):
        shape = (self.plane // 2, LINE, -1, own.shape[-1])
        return self.line_scatter(self.plane_scatter(own.reshape(shape), other.reshape(shape)))

    def total(self, value):
        value = value + self.other(value)
        for bit in range(self.bits):
            value = value + self.swap(value, bit)
        span = 1
        while span < LINE:
            step = span * self.plane
            value = value + self.moved(value, self.pairs(lambda r, g: (r, g ^ step)))
            span = 2 * span
        return value


def dot(left, right):
    return jnp.dot(left, right, preferred_element_type=F32)


def dot_tn(left, right):
    return lax.dot_general(left, right, (((0,), (0,)), ((), ())), preferred_element_type=F32)


def dot_nt(left, right):
    return lax.dot_general(left, right, (((1,), (1,)), ((), ())), preferred_element_type=F32)


def rms_rows(values):
    return lax.rsqrt(jnp.mean(values * values, axis=-1, keepdims=True) + EPSILON)


def norm_back(values, factor, d_base):
    return factor * d_base - values * factor * factor * factor * jnp.mean(
        d_base * values, axis=-1, keepdims=True
    )


def layout(length_row, count):
    pieces = length_row.shape[0]
    earlier = jnp.tril(jnp.ones((pieces, pieces), jnp.int32))
    ends = jnp.sum(earlier * length_row[None, :], axis=1)
    places = jnp.arange(count, dtype=jnp.int32)
    over = (places[:, None] >= ends[None, :]).astype(jnp.int32)
    segment = jnp.sum(over, axis=1)
    return (segment, places - jnp.sum(over * length_row[None, :], axis=1))


def rope_tables(position):
    half = HEAD_DIM // 2
    freq = ROPE_BASE ** (-jnp.arange(half, dtype=F32) * 2.0 / HEAD_DIM)
    angle = position.astype(F32)[:, None] * freq[None, :]
    cosine, sine = (jnp.cos(angle), jnp.sin(angle))
    return (jnp.concatenate([cosine, cosine], axis=1), jnp.concatenate([sine, sine], axis=1))


def rotate(values, cosine, sine):
    half = values.shape[-1] // 2
    turned = jnp.concatenate([-values[..., half:], values[..., :half]], axis=-1)
    return values * cosine[:, None, :] + turned * sine[:, None, :]


def unrotate(grads, cosine, sine):
    half = grads.shape[-1] // 2
    scaled = grads * sine[:, None, :]
    turned = jnp.concatenate([scaled[..., half:], -scaled[..., :half]], axis=-1)
    return grads * cosine[:, None, :] + turned


def scaled_scores(grouped, keys, allowed):
    raw = jnp.einsum("ikgd,jkd->kgij", grouped, keys, preferred_element_type=F32) * HEAD_DIM ** (-0.5)
    return jnp.where(allowed, raw, -1e30)


def wide(row):
    return jnp.pad(row.astype(F32), (0, 128 - row.shape[0]))[None]


def owner_weights(code, weights, numbers, expert):
    code = code.astype(jnp.int32)
    named = (code >> 10) == expert
    order = jnp.sum(jnp.where(named, code & 1023, 0), axis=1)
    weight = jnp.sum(jnp.where(named, weights, 0.0), axis=1)
    has = jnp.any(named, axis=1)
    smaller = has[:, None, :] & (order[:, None, :] < order[:, :, None])
    rank = jnp.sum(smaller.astype(jnp.int32), axis=2)
    count = jnp.sum(has.astype(jnp.int32), axis=1)
    ahead = numbers[None, :] < numbers[:, None]
    before = jnp.sum(jnp.where(ahead, count[None, :], 0), axis=1)
    kept = has & (before[:, None] + rank < CAPACITY)
    return jnp.where(kept, weight, 0.0)


def shards(
    tokens,
    cotangent,
    lengths,
    dealing,
    routes,
    gate_weights,
    pair_order,
    qkv_weight,
    out_weight,
    input_gain,
    query_gain,
    key_gain,
    post_gain,
    gate_weight,
    up_weight,
    down_weight,
):
    wires = Wires()
    count = tokens.shape[0]
    groups, plane = (wires.groups, wires.plane)
    qsize = HEADS * HEAD_DIM
    ksize = KV_HEADS * HEAD_DIM
    ratio = HEADS // KV_HEADS
    qkv_rows, out_rows = (qkv_weight.shape[0], out_weight.shape[0])
    qkv_half, out_half = (qkv_rows // 2, out_rows // 2)
    gathered_rows = plane * count

    small = jnp.concatenate(
        [
            (routes * 1024 + pair_order).astype(F32).T,
            gate_weights.T,
            wide(input_gain),
            wide(post_gain),
            wide(query_gain),
            wide(key_gain),
            jnp.full((1, 128), wires.group, jnp.int32).astype(F32),
            jnp.zeros((3, 128), F32),
        ],
        axis=0,
    )
    small = wires.gather(small)

    def gain_of(row, width):
        found = wires.by_spot(small[:, :, 2 * TOP + row, :width], 1)
        return found.reshape(groups * width)

    gain_one = gain_of(0, input_gain.shape[0])
    gain_two = gain_of(1, post_gain.shape[0])
    gain_query = gain_of(2, query_gain.shape[0])
    gain_key = gain_of(3, key_gain.shape[0])
    flat_small = small.reshape(groups, -1, 128)
    expert_weight = owner_weights(
        flat_small[:, :TOP],
        flat_small[:, TOP : 2 * TOP],
        flat_small[:, 2 * TOP + 4, 0].astype(jnp.int32),
        wires.group,
    ).reshape(groups * count, 1)

    qkv_mine = lax.dynamic_slice_in_dim(qkv_weight, wires.rep * qkv_half, qkv_half, axis=0)
    qkv_line = wires.line_gather(qkv_mine)
    qkv_part = jnp.concatenate([qkv_line, wires.other(qkv_line)], axis=0).reshape(LINE * qkv_rows, -1)
    out_mine = lax.dynamic_slice_in_dim(out_weight, wires.rep * out_half, out_half, axis=0)
    out_line = wires.line_gather(out_mine)
    out_part = jnp.concatenate([out_line, wires.other(out_line)], axis=0).reshape(LINE * out_rows, -1)

    def spread(value, rows):
        blocks = wires.by_relative(value.reshape(count, LINE, plane, rows), 2)
        blocks = wires.plane_swap(blocks).reshape(gathered_rows, LINE, 2, rows // 2)
        return wires.own_first(jnp.moveaxis(blocks, 2, 1), 1).reshape(gathered_rows, LINE * rows)

    def collect(value, rows):
        blocks = wires.own_first(value.reshape(gathered_rows, 2, LINE, rows // 2), 1)
        blocks = jnp.moveaxis(blocks, 1, 2).reshape(plane, count, LINE, rows)
        return wires.by_spot(wires.plane_swap(blocks), 2).reshape(count, LINE * plane * rows)

    def partial_sums(left, weight):
        half = gathered_rows // 2
        other = dot(left[half:], weight).astype(BF16)
        own = dot(left[:half], weight)
        shape = (plane // 2, count, -1)
        return wires.plane_scatter(own.reshape(shape), other.reshape(shape))

    device = lax.axis_index(AXES)
    length_row = jnp.take(lengths, jnp.take(dealing, device), axis=0)
    segment, position = layout(length_row, count)
    cosine, sine = rope_tables(position)
    places = jnp.arange(count, dtype=jnp.int32)
    allowed = (segment[:, None] == segment[None, :]) & (places[None, :] <= places[:, None])

    inputs = tokens.astype(F32)
    scale_in = rms_rows(inputs)
    base_in = inputs * scale_in
    normed = (base_in * gain_one).astype(BF16)
    normed_part = spread(normed, qkv_rows)
    projected = partial_sums(normed_part, qkv_part)

    q_raw = projected[:, :qsize].reshape(count, HEADS, HEAD_DIM)
    k_raw = projected[:, qsize : qsize + ksize].reshape(count, KV_HEADS, HEAD_DIM)
    v_raw = projected[:, qsize + ksize :].reshape(count, KV_HEADS, HEAD_DIM)
    q_scale = rms_rows(q_raw)
    q_base = q_raw * q_scale
    k_scale = rms_rows(k_raw)
    k_base = k_raw * k_scale
    queries = rotate(q_base * gain_query, cosine, sine).astype(BF16)
    keys = rotate(k_base * gain_key, cosine, sine).astype(BF16)
    values = v_raw.astype(BF16)
    grouped = queries.reshape(count, KV_HEADS, ratio, HEAD_DIM)
    scores = scaled_scores(grouped, keys, allowed)
    highest = jnp.max(scores, axis=-1, keepdims=True)
    log_total = highest + jnp.log(jnp.sum(jnp.exp(scores - highest), axis=-1, keepdims=True))
    prob = jnp.exp(scores - log_total)
    mixed = jnp.einsum("kgij,jkd->ikgd", prob.astype(BF16), values, preferred_element_type=F32)
    mixed_low = mixed.reshape(count, qsize).astype(BF16)
    mixed_part = spread(mixed_low, out_rows)
    resid = inputs + partial_sums(mixed_part, out_part)
    scale_post = rms_rows(resid)
    base_post = resid * scale_post
    routed = (base_post * gain_two).astype(BF16)

    gate_local, up_local, down_local = (gate_weight[0], up_weight[0], down_weight[0])

    def experts(rows, cotangents, weights):
        pair_grad = (cotangents.astype(F32) * weights).astype(BF16)
        gate = dot(rows, gate_local)
        upper = dot(rows, up_local)
        d_hidden = dot_nt(pair_grad, down_local)
        sigmoid_gate = jax.nn.sigmoid(gate)
        activated = gate * sigmoid_gate
        hidden = (activated * upper).astype(BF16)
        d_up = (d_hidden * activated).astype(BF16)
        d_gate = (d_hidden * upper * sigmoid_gate * (1.0 + gate * (1.0 - sigmoid_gate))).astype(BF16)
        d_rows = (dot_nt(d_gate, gate_local) + dot_nt(d_up, up_local)).astype(BF16)
        result = dot(hidden, down_local).astype(BF16)
        shares = (result.astype(F32) * weights).astype(BF16)
        sums = (dot_tn(rows, d_gate), dot_tn(rows, d_up), dot_tn(hidden, pair_grad))
        return (d_rows, shares, sums)

    def experts_in_steps(rows, cotangents, weights):
        steps = rows.shape[0] // EXPERT_ROWS
        if steps <= 1:
            return experts(rows, cotangents, weights)

        def step(sums, given):
            d_rows, shares, more = experts(*given)
            return (jax.tree.map(jnp.add, sums, more), (d_rows, shares))

        zeros = (jnp.zeros((D, FF), F32), jnp.zeros((D, FF), F32), jnp.zeros((FF, D), F32))
        given = [value.reshape(steps, EXPERT_ROWS, -1) for value in (rows, cotangents, weights)]
        sums, (d_rows, shares) = lax.scan(step, zeros, tuple(given))
        return (d_rows.reshape(rows.shape), shares.reshape(rows.shape), sums)

    cot_own, cot_other = wires.gather_halves(cotangent)
    routed_own, routed_other = wires.gather_halves(routed)
    weight_own, weight_other = jnp.split(expert_weight, 2, axis=0)
    d_own, shares_own, sums_own = experts_in_steps(routed_own, cot_own, weight_own)
    d_other, shares_other, sums_other = experts_in_steps(routed_other, cot_other, weight_other)
    d_routed = wires.scatter(d_own, d_other)
    output = (resid + wires.scatter(shares_own, shares_other)).astype(BF16)
    gate_total, up_total, down_total = [
        (own + other).astype(BF16) for own, other in zip(sums_own, sums_other)
    ]

    grad_out = cotangent.astype(F32)
    post_total = jnp.sum(d_routed * base_post, axis=0)
    d_resid = grad_out + norm_back(resid, scale_post, d_routed * gain_two)
    d_attn = d_resid.astype(BF16)
    attn_part = wires.plane_gather(d_attn).reshape(gathered_rows, D)
    d_heads = collect(dot_nt(attn_part, out_part).astype(BF16), out_rows)
    d_heads = d_heads.reshape(count, KV_HEADS, ratio, HEAD_DIM)

    def weight_shard(left, right, rows):
        both = dot_tn(left, right).reshape(2, LINE, rows // 2, -1)
        mine = both[0] + wires.other(both[1].astype(BF16)).astype(F32)
        mine = wires.line_scatter(mine)
        pair = jnp.stack([mine, wires.other(mine)], axis=0)
        return wires.own_first(pair, 0).reshape(rows, -1)

    out_shard = weight_shard(mixed_part, attn_part, out_rows)

    prob = jnp.exp(scaled_scores(grouped, keys, allowed) - log_total)
    d_prob = jnp.einsum("ikgd,jkd->kgij", d_heads, values, preferred_element_type=F32)
    d_values = jnp.einsum("kgij,ikgd->jkd", prob.astype(BF16), d_heads, preferred_element_type=F32)
    d_scores = (prob * (d_prob - jnp.sum(prob * d_prob, axis=-1, keepdims=True))).astype(BF16)
    d_grouped = jnp.einsum("kgij,jkd->ikgd", d_scores, keys, preferred_element_type=F32) * HEAD_DIM ** (-0.5)
    d_keys = jnp.einsum("kgij,ikgd->jkd", d_scores, grouped, preferred_element_type=F32) * HEAD_DIM ** (-0.5)
    d_qrot = unrotate(d_grouped.reshape(count, HEADS, HEAD_DIM), cosine, sine)
    d_krot = unrotate(d_keys, cosine, sine)
    query_total = jnp.sum(d_qrot * q_base, axis=(0, 1))
    key_total = jnp.sum(d_krot * k_base, axis=(0, 1))
    d_qraw = norm_back(q_raw, q_scale, d_qrot * gain_query)
    d_kraw = norm_back(k_raw, k_scale, d_krot * gain_key)
    d_projected = jnp.concatenate(
        [
            d_qraw.reshape(count, qsize),
            d_kraw.reshape(count, ksize),
            d_values.reshape(count, ksize),
        ],
        axis=1,
    ).astype(BF16)
    projected_part = wires.plane_gather(d_projected).reshape(gathered_rows, -1)
    qkv_shard = weight_shard(normed_part, projected_part, qkv_rows)
    d_normed = collect(dot_nt(projected_part, qkv_part).astype(BF16), qkv_rows).astype(F32)
    input_total = jnp.sum(d_normed * base_in, axis=0)
    input_grad = d_resid + norm_back(inputs, scale_in, d_normed * gain_one)

    sums = wires.total(jnp.concatenate([input_total, post_total, query_total, key_total]).reshape(-1, 128))
    sums = sums.reshape(-1)

    def sum_shard(start, width):
        return lax.dynamic_slice_in_dim(sums, start + wires.group * width, width)

    def over_replicas(value):
        return (value.astype(F32) + wires.other(value).astype(F32))[None]

    return (
        output,
        input_grad,
        qkv_shard,
        out_shard,
        sum_shard(0, input_gain.shape[0]),
        sum_shard(2 * D, query_gain.shape[0]),
        sum_shard(2 * D + HEAD_DIM, key_gain.shape[0]),
        sum_shard(D, post_gain.shape[0]),
        over_replicas(gate_total),
        over_replicas(up_total),
        over_replicas(down_total),
    )


def solution(mesh):
    both, one = (P(AXES, None), P("grp"))
    rows, experts = (P("grp", None), P("grp", None, None))
    return jax.shard_map(
        shards,
        mesh=mesh,
        in_specs=(both, both, P(), P(), both, both, both, rows, rows, one, one, one, one, experts, experts, experts),
        out_specs=(both, both, rows, rows, one, one, one, one, experts, experts, experts),
        check_vma=False,
    )
```

```python
import jax
import jax.numpy as jnp
from jax import lax
from jax.sharding import PartitionSpec as P

D = 2048
HEADS = 32
KV_HEADS = 4
HEAD_DIM = 128
FF = 768
TOP = 8
CAPACITY = 1280
LINE = 4
EXPERT_ROWS = 1024

EPSILON = 1e-06
ROPE_BASE = 1000000.0
AXES = ("rep", "grp")
F32 = jnp.float32
BF16 = jnp.bfloat16


class Wires:
    def __init__(self):
        self.groups = lax.axis_size("grp")
        self.plane = self.groups // LINE
        self.bits = self.plane.bit_length() - 1
        self.rep = lax.axis_index("rep")
        self.group = lax.axis_index("grp")
        self.line = self.group // self.plane
        self.spot = self.group % self.plane

    def moved(self, value, pairs):
        return lax.ppermute(value, AXES, pairs)

    def pairs(self, where):
        found = []
        for r in range(2):
            for g in range(self.groups):
                to = where(r, g)
                if to is not None:
                    found.append((r * self.groups + g, to[0] * self.groups + to[1]))
        return found

    def swap(self, value, bit):
        last = self.bits - 1
        return self.moved(value, self.pairs(lambda r, g: (r, g ^ (1 << (bit if r == 0 else last - bit)))))

    def other(self, value):
        return self.moved(value, self.pairs(lambda r, g: (1 - r, g)))

    def along(self, value, step, first, final):
        def to(r, g):
            here = g // self.plane
            if first <= here <= final:
                return (r, g + step * self.plane)
            return None

        return self.moved(value, self.pairs(to))

    def line_gather(self, value):
        lower, upper = [value], [value]
        for t in range(1, LINE):
            lower.append(self.along(lower[-1], 1, t - 1, LINE - 2))
            upper.append(self.along(upper[-1], -1, 1, LINE - t))
        row = jnp.stack(lower[:0:-1] + upper, axis=0)
        return lax.dynamic_slice_in_dim(row, LINE - 1 - self.line, LINE, axis=0)

    def line_scatter(self, value):
        def piece(j):
            place = jnp.clip(self.line + j, 0, LINE - 1)
            return lax.dynamic_index_in_dim(value, place, 0, keepdims=False).astype(F32)

        total = piece(0)
        for way in (1, -1):
            carried = None
            for t in range(LINE - 1, 0, -1):
                part = piece(way * t)
                if carried is not None:
                    part = part + carried
                if way == 1:
                    first, final = (0, LINE - 1 - t)
                else:
                    first, final = (t, LINE - 1)
                carried = self.along(part.astype(BF16), way, first, final).astype(F32)
            total = total + carried
        return total

    def plane_gather(self, value):
        for bit in range(self.bits):
            value = jnp.stack([value, self.swap(value, bit)], axis=0)
        return value.reshape((self.plane,) + value.shape[self.bits :])

    def plane_scatter(self, own, other):
        for bit in reversed(range(self.bits)):
            arrived = self.swap(other.astype(BF16), bit)
            value = own.astype(F32) + arrived.astype(F32)
            half = value.shape[0] // 2
            own, other = (value[:half], value[half:])
        return value[0]

    def plane_swap(self, value):
        rest = value.shape[1:]
        value = value.reshape((2,) * self.bits + rest)
        for bit in range(self.bits):
            axis = self.bits - 1 - bit
            kept = lax.index_in_dim(value, 0, axis, keepdims=False)
            sent = lax.index_in_dim(value, 1, axis, keepdims=False)
            value = jnp.stack([kept, self.swap(sent, bit)], axis=axis)
        return value.reshape((self.plane,) + rest)

    def turned(self, number):
        back = sum(((number >> i) & 1) << (self.bits - 1 - i) for i in range(self.bits))
        return jnp.where(self.rep == 0, number, back)

    def both(self, mine, other, axis):
        first = jnp.where(self.rep == 0, mine, other)
        second = jnp.where(self.rep == 0, other, mine)
        return jnp.stack([first, second], axis=axis)

    def by_relative(self, blocks):
        width = blocks.shape[1] // self.groups
        found = []
        for k in range(self.plane):
            spot = self.spot ^ self.turned(k)
            pieces = [
                lax.dynamic_slice_in_dim(blocks, (at * self.plane + spot) * width, width, axis=1)
                for at in range(LINE)
            ]
            found.append(jnp.concatenate(pieces, axis=1))
        return jnp.stack(found, axis=0)

    def by_spot(self, blocks):
        width = blocks.shape[2] // LINE
        found = [
            lax.dynamic_index_in_dim(blocks, self.turned(self.spot ^ q), 0, keepdims=False)
            for q in range(self.plane)
        ]
        pieces = [found[q][:, at * width : (at + 1) * width] for at in range(LINE) for q in range(self.plane)]
        return jnp.concatenate(pieces, axis=1)

    def gather(self, value):
        return self.plane_gather(self.line_gather(value))

    def gather_halves(self, value, lined=False):
        value = value if lined else self.line_gather(value)
        for bit in range(self.bits - 1):
            value = jnp.concatenate([value, self.swap(value, bit)], axis=0)
        value = value.reshape(-1, value.shape[-1])
        return (value, self.swap(value, self.bits - 1))

    def scatter(self, own, other):
        shape = (self.plane // 2, LINE, -1, own.shape[-1])
        return self.line_scatter(self.plane_scatter(own.reshape(shape), other.reshape(shape)))

    def total(self, value):
        value = value + self.other(value)
        for bit in range(self.bits):
            value = value + self.swap(value, bit)
        span = 1
        while span < LINE:
            step = span * self.plane
            value = value + self.moved(value, self.pairs(lambda r, g: (r, g ^ step)))
            span = 2 * span
        return value


def dot(left, right):
    return jnp.dot(left, right, preferred_element_type=F32)


def dot_tn(left, right):
    return lax.dot_general(left, right, (((0,), (0,)), ((), ())), preferred_element_type=F32)


def dot_nt(left, right):
    return lax.dot_general(left, right, (((1,), (1,)), ((), ())), preferred_element_type=F32)


def rms_rows(values):
    return lax.rsqrt(jnp.mean(values * values, axis=-1, keepdims=True) + EPSILON)


def norm_back(values, factor, d_base):
    return factor * d_base - values * factor * factor * factor * jnp.mean(
        d_base * values, axis=-1, keepdims=True
    )


def layout(length_row, count):
    pieces = length_row.shape[0]
    earlier = jnp.tril(jnp.ones((pieces, pieces), jnp.int32))
    ends = jnp.sum(earlier * length_row[None, :], axis=1)
    places = jnp.arange(count, dtype=jnp.int32)
    over = (places[:, None] >= ends[None, :]).astype(jnp.int32)
    segment = jnp.sum(over, axis=1)
    return (segment, places - jnp.sum(over * length_row[None, :], axis=1))


def rope_tables(position):
    half = HEAD_DIM // 2
    freq = ROPE_BASE ** (-jnp.arange(half, dtype=F32) * 2.0 / HEAD_DIM)
    angle = position.astype(F32)[:, None] * freq[None, :]
    cosine, sine = (jnp.cos(angle), jnp.sin(angle))
    return (jnp.concatenate([cosine, cosine], axis=1), jnp.concatenate([sine, sine], axis=1))


def rotate(values, cosine, sine):
    half = values.shape[-1] // 2
    turned = jnp.concatenate([-values[..., half:], values[..., :half]], axis=-1)
    return values * cosine[:, None, :] + turned * sine[:, None, :]


def unrotate(grads, cosine, sine):
    half = grads.shape[-1] // 2
    scaled = grads * sine[:, None, :]
    turned = jnp.concatenate([scaled[..., half:], -scaled[..., :half]], axis=-1)
    return grads * cosine[:, None, :] + turned


def scaled_scores(grouped, keys, allowed):
    raw = jnp.einsum("ikgd,jkd->kgij", grouped, keys, preferred_element_type=F32) * HEAD_DIM ** (-0.5)
    return jnp.where(allowed, raw, -1e30)


def wide(row):
    return jnp.pad(row.astype(F32), (0, 128 - row.shape[0]))[None]


def owner_weights(code, weights, numbers, expert):
    code = code.astype(jnp.int32)
    named = (code >> 10) == expert
    order = jnp.sum(jnp.where(named, code & 1023, 0), axis=1)
    weight = jnp.sum(jnp.where(named, weights, 0.0), axis=1)
    has = jnp.any(named, axis=1)
    smaller = has[:, None, :] & (order[:, None, :] < order[:, :, None])
    rank = jnp.sum(smaller.astype(jnp.int32), axis=2)
    count = jnp.sum(has.astype(jnp.int32), axis=1)
    ahead = numbers[None, :] < numbers[:, None]
    before = jnp.sum(jnp.where(ahead, count[None, :], 0), axis=1)
    kept = has & (before[:, None] + rank < CAPACITY)
    return jnp.where(kept, weight, 0.0)


def shards(
    tokens,
    cotangent,
    lengths,
    dealing,
    routes,
    gate_weights,
    pair_order,
    qkv_weight,
    out_weight,
    input_gain,
    query_gain,
    key_gain,
    post_gain,
    gate_weight,
    up_weight,
    down_weight,
):
    wires = Wires()
    count = tokens.shape[0]
    groups, plane = (wires.groups, wires.plane)
    qsize = HEADS * HEAD_DIM
    ksize = KV_HEADS * HEAD_DIM
    ratio = HEADS // KV_HEADS
    qkv_rows, out_rows = (qkv_weight.shape[0], out_weight.shape[0])
    qkv_half, out_half = (qkv_rows // 2, out_rows // 2)
    gathered_rows = plane * count

    small = jnp.concatenate(
        [
            (routes * 1024 + pair_order).astype(F32).T,
            gate_weights.T,
            wide(input_gain),
            wide(post_gain),
            wide(query_gain),
            wide(key_gain),
            jnp.full((1, 128), wires.group, jnp.int32).astype(F32),
            jnp.zeros((3, 128), F32),
        ],
        axis=0,
    )
    small = wires.gather(small)

    def gain_of(row, width):
        row = small[:, :, 2 * TOP + row, :width].reshape(plane, 1, LINE * width)
        return wires.by_spot(row).reshape(groups * width)

    gain_one = gain_of(0, input_gain.shape[0])
    gain_two = gain_of(1, post_gain.shape[0])
    gain_query = gain_of(2, query_gain.shape[0])
    gain_key = gain_of(3, key_gain.shape[0])
    flat_small = small.reshape(groups, -1, 128)
    expert_weight = owner_weights(
        flat_small[:, :TOP],
        flat_small[:, TOP : 2 * TOP],
        flat_small[:, 2 * TOP + 4, 0].astype(jnp.int32),
        wires.group,
    ).reshape(groups * count, 1)

    qkv_mine = lax.dynamic_slice_in_dim(qkv_weight, wires.rep * qkv_half, qkv_half, axis=0)
    qkv_line = wires.line_gather(qkv_mine)
    qkv_part = wires.both(qkv_line, wires.other(qkv_line), 1).reshape(LINE * qkv_rows, -1)
    out_mine = lax.dynamic_slice_in_dim(out_weight, wires.rep * out_half, out_half, axis=0)
    out_line = wires.line_gather(out_mine)
    out_part = wires.both(out_line, wires.other(out_line), 1).reshape(LINE * out_rows, -1)

    def spread(value, rows):
        return wires.plane_swap(wires.by_relative(value)).reshape(gathered_rows, LINE * rows)

    def collect(value, rows):
        return wires.by_spot(wires.plane_swap(value.reshape(plane, count, LINE * rows)))

    def partial_sums(left, weight):
        half = gathered_rows // 2
        other = dot(left[half:], weight).astype(BF16)
        own = dot(left[:half], weight)
        shape = (plane // 2, count, -1)
        return wires.plane_scatter(own.reshape(shape), other.reshape(shape))

    device = lax.axis_index(AXES)
    length_row = jnp.take(lengths, jnp.take(dealing, device), axis=0)
    segment, position = layout(length_row, count)
    cosine, sine = rope_tables(position)
    places = jnp.arange(count, dtype=jnp.int32)
    allowed = (segment[:, None] == segment[None, :]) & (places[None, :] <= places[:, None])

    inputs = tokens.astype(F32)
    scale_in = rms_rows(inputs)
    base_in = inputs * scale_in
    normed = (base_in * gain_one).astype(BF16)
    normed_part = spread(normed, qkv_rows)
    cot_line = wires.line_gather(cotangent)
    cot_line, normed_part = lax.optimization_barrier((cot_line, normed_part))
    projected = partial_sums(normed_part, qkv_part)
    cot_own, cot_other = wires.gather_halves(cot_line, lined=True)

    q_raw = projected[:, :qsize].reshape(count, HEADS, HEAD_DIM)
    k_raw = projected[:, qsize : qsize + ksize].reshape(count, KV_HEADS, HEAD_DIM)
    v_raw = projected[:, qsize + ksize :].reshape(count, KV_HEADS, HEAD_DIM)
    q_scale = rms_rows(q_raw)
    q_base = q_raw * q_scale
    k_scale = rms_rows(k_raw)
    k_base = k_raw * k_scale
    queries = rotate(q_base * gain_query, cosine, sine).astype(BF16)
    keys = rotate(k_base * gain_key, cosine, sine).astype(BF16)
    values = v_raw.astype(BF16)
    grouped = queries.reshape(count, KV_HEADS, ratio, HEAD_DIM)
    scores = scaled_scores(grouped, keys, allowed)
    highest = jnp.max(scores, axis=-1, keepdims=True)
    log_total = highest + jnp.log(jnp.sum(jnp.exp(scores - highest), axis=-1, keepdims=True))
    prob = jnp.exp(scores - log_total)
    mixed = jnp.einsum("kgij,jkd->ikgd", prob.astype(BF16), values, preferred_element_type=F32)
    mixed_low = mixed.reshape(count, qsize).astype(BF16)
    mixed_part = spread(mixed_low, out_rows)
    cot_own, cot_other, mixed_part = lax.optimization_barrier((cot_own, cot_other, mixed_part))
    resid = inputs + partial_sums(mixed_part, out_part)
    scale_post = rms_rows(resid)
    base_post = resid * scale_post
    routed = (base_post * gain_two).astype(BF16)

    gate_local, up_local, down_local = (gate_weight[0], up_weight[0], down_weight[0])

    def experts(rows, cotangents, weights):
        pair_grad = (cotangents.astype(F32) * weights).astype(BF16)
        gate = dot(rows, gate_local)
        upper = dot(rows, up_local)
        d_hidden = dot_nt(pair_grad, down_local)
        sigmoid_gate = jax.nn.sigmoid(gate)
        activated = gate * sigmoid_gate
        hidden = (activated * upper).astype(BF16)
        d_up = (d_hidden * activated).astype(BF16)
        d_gate = (d_hidden * upper * sigmoid_gate * (1.0 + gate * (1.0 - sigmoid_gate))).astype(BF16)
        d_rows = (dot_nt(d_gate, gate_local) + dot_nt(d_up, up_local)).astype(BF16)
        result = dot(hidden, down_local).astype(BF16)
        shares = (result.astype(F32) * weights).astype(BF16)
        sums = (dot_tn(rows, d_gate), dot_tn(rows, d_up), dot_tn(hidden, pair_grad))
        return (d_rows, shares, sums)

    def experts_in_steps(rows, cotangents, weights):
        steps = rows.shape[0] // EXPERT_ROWS
        if steps <= 1:
            return experts(rows, cotangents, weights)

        def step(sums, given):
            d_rows, shares, more = experts(*given)
            return (jax.tree.map(jnp.add, sums, more), (d_rows, shares))

        zeros = (jnp.zeros((D, FF), F32), jnp.zeros((D, FF), F32), jnp.zeros((FF, D), F32))
        given = [value.reshape(steps, EXPERT_ROWS, -1) for value in (rows, cotangents, weights)]
        sums, (d_rows, shares) = lax.scan(step, zeros, tuple(given))
        return (d_rows.reshape(rows.shape), shares.reshape(rows.shape), sums)

    routed_own, routed_other = wires.gather_halves(routed)
    weight_own, weight_other = jnp.split(expert_weight, 2, axis=0)
    d_own, shares_own, sums_own = experts_in_steps(routed_own, cot_own, weight_own)
    d_other, shares_other, sums_other = experts_in_steps(routed_other, cot_other, weight_other)
    d_routed = wires.scatter(d_own, d_other)
    output = (resid + wires.scatter(shares_own, shares_other)).astype(BF16)
    gate_total, up_total, down_total = [
        (own + other).astype(BF16) for own, other in zip(sums_own, sums_other)
    ]

    grad_out = cotangent.astype(F32)
    post_total = jnp.sum(d_routed * base_post, axis=0)
    d_resid = grad_out + norm_back(resid, scale_post, d_routed * gain_two)
    d_attn = d_resid.astype(BF16)
    attn_part = wires.plane_gather(d_attn).reshape(gathered_rows, D)
    d_heads = collect(dot_nt(attn_part, out_part).astype(BF16), out_rows)
    d_heads = d_heads.reshape(count, KV_HEADS, ratio, HEAD_DIM)

    def weight_shard(left, right, rows):
        both = dot_tn(left, right).reshape(LINE, 2, rows // 2, -1)
        mine = lax.dynamic_index_in_dim(both, wires.rep, 1, keepdims=False)
        theirs = lax.dynamic_index_in_dim(both, 1 - wires.rep, 1, keepdims=False)
        mine = wires.line_scatter(mine + wires.other(theirs.astype(BF16)).astype(F32))
        return wires.both(mine, wires.other(mine), 0).reshape(rows, -1)

    out_shard = weight_shard(mixed_part, attn_part, out_rows)

    prob = jnp.exp(scaled_scores(grouped, keys, allowed) - log_total)
    d_prob = jnp.einsum("ikgd,jkd->kgij", d_heads, values, preferred_element_type=F32)
    d_values = jnp.einsum("kgij,ikgd->jkd", prob.astype(BF16), d_heads, preferred_element_type=F32)
    d_scores = (prob * (d_prob - jnp.sum(prob * d_prob, axis=-1, keepdims=True))).astype(BF16)
    d_grouped = jnp.einsum("kgij,jkd->ikgd", d_scores, keys, preferred_element_type=F32) * HEAD_DIM ** (-0.5)
    d_keys = jnp.einsum("kgij,ikgd->jkd", d_scores, grouped, preferred_element_type=F32) * HEAD_DIM ** (-0.5)
    d_qrot = unrotate(d_grouped.reshape(count, HEADS, HEAD_DIM), cosine, sine)
    d_krot = unrotate(d_keys, cosine, sine)
    query_total = jnp.sum(d_qrot * q_base, axis=(0, 1))
    key_total = jnp.sum(d_krot * k_base, axis=(0, 1))
    d_qraw = norm_back(q_raw, q_scale, d_qrot * gain_query)
    d_kraw = norm_back(k_raw, k_scale, d_krot * gain_key)
    d_projected = jnp.concatenate(
        [
            d_qraw.reshape(count, qsize),
            d_kraw.reshape(count, ksize),
            d_values.reshape(count, ksize),
        ],
        axis=1,
    ).astype(BF16)
    projected_part = wires.plane_gather(d_projected).reshape(gathered_rows, -1)
    qkv_shard = weight_shard(normed_part, projected_part, qkv_rows)
    d_normed = collect(dot_nt(projected_part, qkv_part).astype(BF16), qkv_rows).astype(F32)
    input_total = jnp.sum(d_normed * base_in, axis=0)
    input_grad = d_resid + norm_back(inputs, scale_in, d_normed * gain_one)

    sums = wires.total(jnp.concatenate([input_total, post_total, query_total, key_total]).reshape(-1, 128))
    sums = sums.reshape(-1)

    def sum_shard(start, width):
        return lax.dynamic_slice_in_dim(sums, start + wires.group * width, width)

    def over_replicas(value):
        return (value.astype(F32) + wires.other(value).astype(F32))[None]

    return (
        output,
        input_grad,
        qkv_shard,
        out_shard,
        sum_shard(0, input_gain.shape[0]),
        sum_shard(2 * D, query_gain.shape[0]),
        sum_shard(2 * D + HEAD_DIM, key_gain.shape[0]),
        sum_shard(D, post_gain.shape[0]),
        over_replicas(gate_total),
        over_replicas(up_total),
        over_replicas(down_total),
    )


def solution(mesh):
    both, one = (P(AXES, None), P("grp"))
    rows, experts = (P("grp", None), P("grp", None, None))
    return jax.shard_map(
        shards,
        mesh=mesh,
        in_specs=(both, both, P(), P(), both, both, both, rows, rows, one, one, one, one, experts, experts, experts),
        out_specs=(both, both, rows, rows, one, one, one, one, experts, experts, experts),
        check_vma=False,
    )
```
